512 devices in a mesh: shot: 8 (over z_hi, x), recv: 8 (over y), surf: 8 (over z_lo, core).
Axes of the slice: x: 4, y: 8, z: 8 (z_hi: 2, z_lo: 4; z = z_hi * 4 + z_lo), core: 2. Of those that a mesh axis runs over, the one named last changes fastest.
Arguments:
- shot_data: bfloat16 [8, 2, 6144, 2048], P(None, None, ('surf', 'recv'), 'shot'), may hold values from -6 to 6
- recv_data: bfloat16 [8, 2, 6144, 2048], P(None, None, ('surf', 'shot'), 'recv'), may hold values from -0.078125 to 0.078125
- shot_offset: int32 [2048], P('shot'), may hold values from -256 to 255
- recv_offset: int32 [2048], P('recv'), may hold values from -256 to 255
- shot_taper_index: int32 [2048], P('shot'), may hold values from 0 to 3
- receiver_taper_index: int32 [2048], P('recv'), may hold values from 0 to 3
Outputs:
- predicted: float32 [8, 2, 2048, 2048], P('surf', None, 'shot', 'recv')
The draws below stay inside these ranges and needn't reach their ends.
All inputs are finite; a program needn't handle non-finite values.
Results may differ from the reference program's by a relative error of at most 0.0003.
Values may be sent and summed in bfloat16 or wider, within the bound.
A program may use at most 64 MiB of HBM per device.

```python
import jax
import jax.numpy as jnp
from jax import lax

S = 2048
R = 2048
K = 6144
FREQS = 8


def plant(values, key, least, high):
    longest = values.shape.index(max(values.shape))
    spots = []
    for shift in (0, 1):
        where = [jax.random.randint(jax.random.fold_in(key, axis), (), 0, length) for axis, length in enumerate(values.shape)]
        where[longest] = (where[longest] + shift) % values.shape[longest]
        spots.append(tuple(where))
    return values.at[spots[0]].set(least).at[spots[1]].set(high)


def strengthened(values, rng, source, target, blocks, factor):
    def block_of(position):
        return (jnp.arange(values.shape[position]) // (values.shape[position] // blocks)).reshape((-1,) + (1,) * (values.ndim - 1 - position))

    one_side = jax.random.permutation(rng, blocks)[block_of(target)]
    far = (block_of(target) + blocks // 2) % blocks
    return jnp.where((block_of(source) == one_side) | (block_of(source) == far), factor * values, values)


def levels(rng, shape, shards, low, high):
    gain, own = 1.0, jax.random.fold_in(rng, 6)
    for dim, shards_of in shards:
        heights = jnp.exp(jax.random.uniform(jax.random.fold_in(own, dim), (shards_of,), jnp.float32, low / len(shards), high / len(shards)))
        gain = gain * jnp.repeat(heights, shape[dim] // shards_of).reshape([-1 if axis == dim else 1 for axis in range(len(shape))])
    return gain


def scatter_about(rng, shape, spread, most, cuts=(), kind=jnp.bfloat16):
    gain = levels(rng, shape, cuts, -0.22, 0.18) if cuts else 1.0
    array = jax.random.normal(rng, shape, jnp.float32) * spread * gain
    return jnp.minimum(jnp.maximum(array, -most), most).astype(kind)


def gaussian_with(rng, extent, scale, limit, cuts, heavy, kind=jnp.bfloat16):
    array = scale * jax.random.normal(rng, extent, jnp.float32)
    if cuts:
        array = array * levels(rng, extent, cuts, -0.22, 0.18)
    return jnp.clip(strengthened(array, jax.random.fold_in(rng, 3), *heavy), -limit, limit).astype(kind)


def setup_inputs(seed: int = 0) -> dict:
    seeds = jax.random.split(jax.random.key(seed), 7)
    shot_data = scatter_about(seeds[0], (FREQS, 2, K, S), 1.0, 6.0, ((2, 64), (3, 8)))
    recv_data = gaussian_with(seeds[1], (FREQS, 2, K, R), (2 * K) ** -0.5, 0.078125, ((2, 64), (3, 8)), (2, 0, 8, 2.0))
    shot_offset = plant(jax.random.randint(seeds[2], (S,), 0 - R // 8, R // 8), jax.random.fold_in(seeds[2], 1), 0 - R // 8, (R // 8) - 1).astype(jnp.int32)
    recv_offset = plant(jax.random.randint(seeds[3], (R,), 0 - R // 8, R // 8), jax.random.fold_in(seeds[3], 1), 0 - R // 8, (R // 8) - 1).astype(jnp.int32)
    shot_taper_index = plant(jax.random.randint(seeds[4], (S,), 0, 4), jax.random.fold_in(seeds[4], 1), 0, 3).astype(jnp.int32)
    receiver_taper_index = plant(jax.random.randint(seeds[5], (R,), 0, 4), jax.random.fold_in(seeds[5], 1), 0, 3).astype(jnp.int32)
    return {"shot_data": shot_data, "recv_data": recv_data, "shot_offset": shot_offset, "recv_offset": recv_offset, "shot_taper_index": shot_taper_index, "receiver_taper_index": receiver_taper_index}


def frequency_slice_product(pair):
    left_operand, right_operand = pair
    real_real = jnp.dot(left_operand[0].T, right_operand[0], preferred_element_type=jnp.float32)
    imag_imag = jnp.dot(left_operand[1].T, right_operand[1], preferred_element_type=jnp.float32)
    real_imag = jnp.dot(left_operand[0].T, right_operand[1], preferred_element_type=jnp.float32)
    imag_real = jnp.dot(left_operand[1].T, right_operand[0], preferred_element_type=jnp.float32)
    return jnp.stack([real_real - imag_imag, real_imag + imag_real], axis=0)


def reference(shot_data, recv_data, shot_offset, recv_offset, shot_taper_index, receiver_taper_index):
    multiples = lax.map(frequency_slice_product, (shot_data, recv_data))
    shot_pos = jnp.arange(S, dtype=jnp.int32) + shot_offset
    recv_pos = jnp.arange(R, dtype=jnp.int32) + recv_offset
    distance = jnp.abs(recv_pos[None, :] - shot_pos[:, None])
    half_width = (R // 8) * (2 + shot_taper_index[:, None] + receiver_taper_index[None, :])
    ratio = jnp.minimum(distance, half_width).astype(jnp.float32) / half_width.astype(jnp.float32)
    taper = 0.5 * (1.0 + jnp.cos(jnp.pi * ratio))
    return multiples * taper[None, None, :, :]
```

```python
import jax
import jax.numpy as jnp
from jax import lax
from jax.experimental import pallas as pl
from jax.experimental.pallas import tpu as pltpu
from jax.sharding import PartitionSpec as P

R = 2048
MESH = pl.DeviceIdType.MESH
NEAR = ((0, 0), (0, 1), (1, 0), (1, 1), (3, 0), (3, 1), (2, 0), (2, 1))
FAR = ((2, 0), (2, 1), (3, 0), (3, 1), (1, 0), (1, 1), (0, 0), (0, 1))


def kernel(s_ref, r_ref, out_ref, a_buf, b_buf, acc, a_sem, b_sem, sa_sem, sb_sem, yr_sem, yl_sem, xr_sem, xl_sem):
    shot = lax.axis_index("shot")
    y = lax.axis_index("recv")
    u = lax.axis_index("surf")
    zh, x = shot // 4, shot % 4
    zl, c = u // 2, u % 2
    rows = s_ref.shape[2]
    half = 4 * rows

    def surf_of(step):
        b, e = step
        return ((zl + b) % 4) * 2 + (c + e) % 2

    def dest_of(step):
        b, e = step
        return ((zl + 4 - b) % 4) * 2 + (c + e) % 2

    def a_at(v, origin):
        return a_buf.at[v, :, pl.ds(pl.multiple_of(origin * rows, rows), rows), :]

    def b_at(v, origin):
        return b_buf.at[v, :, pl.ds(pl.multiple_of(origin * rows, rows), rows), :]

    def s_of(h, xx):
        return h * 4 + xx

    right = {"recv": (y + 1) % 8}
    left = {"recv": (y + 7) % 8}
    xright = {"shot": s_of(zh, (x + 1) % 4)}
    xleft = {"shot": s_of(zh, (x + 3) % 4)}
    other = s_of(1 - zh, x)

    barrier = pltpu.get_barrier_semaphore()
    peers = [right, left, xright, xleft]
    for step in NEAR:
        f = dest_of(step)
        if step != (0, 0):
            peers.append({"surf": f})
        peers.append({"shot": other, "surf": f})
    for peer in peers:
        pl.semaphore_signal(barrier, inc=1, device_id=peer, device_id_type=MESH)
    pl.semaphore_wait(barrier, len(peers))

    started = []

    def send(src, dst, send_sem, recv_sem, device):
        copy = pltpu.make_async_remote_copy(
            src_ref=src, dst_ref=dst, send_sem=send_sem, recv_sem=recv_sem, device_id=device, device_id_type=MESH
        )
        copy.start()
        started.append(copy)

    for i in range(8):
        if i == 0:
            pltpu.make_async_copy(s_ref.at[u], a_at(u, y), a_sem.at[u, y]).start()
            pltpu.make_async_copy(r_ref.at[u], b_at(u, shot), b_sem.at[u, shot]).start()
        else:
            f = dest_of(NEAR[i])
            send(s_ref.at[f], a_at(u, y), sa_sem.at[i], a_sem.at[u, y], {"surf": f})
            send(r_ref.at[f], b_at(u, shot), sb_sem.at[i], b_sem.at[u, shot], {"surf": f})
        f = dest_of(FAR[i])
        send(r_ref.at[f], b_at(u, shot), sb_sem.at[8 + i], b_sem.at[u, shot], {"shot": other, "surf": f})

    def a_wait(v, origin):
        pltpu.make_async_copy(a_at(v, origin), a_at(v, origin), a_sem.at[v, origin]).wait()

    def b_wait(v, origin):
        pltpu.make_async_copy(b_at(v, origin), b_at(v, origin), b_sem.at[v, origin]).wait()

    def a_right(v, origin):
        send(a_at(v, origin), a_at(v, origin), yr_sem.at[v, origin], a_sem.at[v, origin], right)

    def a_left(v, origin):
        send(a_at(v, origin), a_at(v, origin), yl_sem.at[v, origin], a_sem.at[v, origin], left)

    def b_right(v, origin):
        send(b_at(v, origin), b_at(v, origin), xr_sem.at[v, origin], b_sem.at[v, origin], xright)

    def b_left(v, origin):
        send(b_at(v, origin), b_at(v, origin), xl_sem.at[v, origin], b_sem.at[v, origin], xleft)

    def dot(v, h, ca, cb):
        here = pl.ds(pl.multiple_of(h * half, half), half)
        return lax.dot_general(
            a_buf[v, ca, here, :], b_buf[v, cb, here, :], (((0,), (0,)), ((), ())), preferred_element_type=jnp.float32
        )

    acc[...] = jnp.zeros_like(acc)

    def multiply(v, h):
        acc[0] += dot(v, h, 0, 0) - dot(v, h, 1, 1)
        acc[1] += dot(v, h, 0, 1) + dot(v, h, 1, 0)

    def b_pass(v, h, flip):
        if flip:
            b_wait(v, s_of(h, (x + 1) % 4))
            b_left(v, s_of(h, (x + 1) % 4))
        else:
            b_wait(v, s_of(h, (x + 3) % 4))
            b_right(v, s_of(h, (x + 3) % 4))

    def b_finish(v, h, flip):
        b_wait(v, s_of(h, (x + 3) % 4) if flip else s_of(h, (x + 1) % 4))
        b_wait(v, s_of(h, (x + 2) % 4))

    for t in range(12):
        if t < 8:
            v = surf_of(NEAR[t])
            a_wait(v, y)
            a_right(v, y)
            a_left(v, y)
            b_wait(v, shot)
            b_right(v, shot)
            b_left(v, shot)
            w = surf_of(FAR[t])
            b_wait(w, other)
            b_right(w, other)
            b_left(w, other)
        for lag in (1, 2, 3):
            q = t - lag
            if not 0 <= q < 8:
                continue
            v = surf_of(NEAR[q])
            before, after = (y + 8 - lag) % 8, (y + lag) % 8
            a_wait(v, before)
            if lag < 3 or q % 2 == 0:
                a_right(v, before)
            a_wait(v, after)
            if lag < 3 or q % 2 == 1:
                a_left(v, after)
            if lag == 1:
                b_pass(v, zh, q % 2 == 1)
                b_pass(surf_of(FAR[q]), 1 - zh, q % 2 == 0)
        q = t - 4
        if q >= 0:
            v = surf_of(NEAR[q])
            a_wait(v, (y + 4) % 8)
            b_finish(v, zh, q % 2 == 1)
            multiply(v, zh)
            b_finish(surf_of(FAR[q]), 1 - zh, q % 2 == 0)
            for m in range(8):
                if max(m, NEAR.index(FAR[m])) == q:
                    multiply(surf_of(FAR[m]), 1 - zh)
    out_ref[...] = acc[...]
    for copy in started:
        copy.wait_send()


def products(shot_data, recv_data):
    freqs, parts, rows, cols = shot_data.shape
    dma = pltpu.SemaphoreType.DMA
    return pl.pallas_call(
        kernel,
        out_shape=jax.ShapeDtypeStruct((parts, cols, cols), jnp.float32),
        in_specs=[pl.BlockSpec(memory_space=pl.ANY)] * 2,
        out_specs=pl.BlockSpec(memory_space=pltpu.VMEM),
        scratch_shapes=[
            pltpu.VMEM((freqs, parts, 8 * rows, cols), shot_data.dtype),
            pltpu.VMEM((freqs, parts, 8 * rows, cols), shot_data.dtype),
            pltpu.VMEM((parts, cols, cols), jnp.float32),
            dma((8, 8)),
            dma((8, 8)),
            dma((8,)),
            dma((16,)),
            dma((8, 8)),
            dma((8, 8)),
            dma((8, 8)),
            dma((8, 8)),
        ],
        compiler_params=pltpu.CompilerParams(
            collective_id=0, has_side_effects=True, vmem_limit_bytes=40 * 1024 * 1024
        ),
    )(shot_data, recv_data)


def on_device(shot_data, recv_data, shot_offset, recv_offset, shot_taper_index, receiver_taper_index):
    multiples = products(shot_data, recv_data)
    shot_row_block = shot_offset.shape[0]
    recv_cols = recv_offset.shape[0]
    shot_pos = (
        lax.axis_index("shot") * shot_row_block
        + jnp.arange(shot_row_block, dtype=jnp.int32)
        + shot_offset
    )
    recv_pos = (
        lax.axis_index("recv") * recv_cols + jnp.arange(recv_cols, dtype=jnp.int32) + recv_offset
    )
    distance = jnp.abs(recv_pos[None, :] - shot_pos[:, None])
    half_width = R // 8 * (2 + shot_taper_index[:, None] + receiver_taper_index[None, :])
    ratio = jnp.minimum(distance, half_width).astype(jnp.float32) / half_width.astype(jnp.float32)
    taper = 0.5 * (1.0 + jnp.cos(jnp.pi * ratio))
    return (multiples * taper[None, :, :])[None]


def solution(mesh):
    placed = (
        P(None, None, ("surf", "recv"), "shot"),
        P(None, None, ("surf", "shot"), "recv"),
        P("shot"),
        P("recv"),
        P("shot"),
        P("recv"),
    )
    return jax.shard_map(
        on_device,
        mesh=mesh,
        in_specs=placed,
        out_specs=P("surf", None, "shot", "recv"),
        check_vma=False,
    )
```

```python
import jax
import jax.numpy as jnp
from jax import lax
from jax.experimental import pallas as pl
from jax.experimental.pallas import tpu as pltpu
from jax.sharding import PartitionSpec as P

NEAR = ((0, 0), (0, 1), (1, 0), (1, 1), (2, 0), (2, 1), (3, 0), (3, 1))
FAR = ((2, 0), (2, 1), (3, 0), (3, 1), (1, 0), (1, 1), (0, 0), (0, 1))
PROGRAM = (
    ('S', 0), ('S', 1), ('N', 1), ('F', 0), ('S', 2), ('S', 3), ('F', 1), ('S', 4),
    ('S', 5), ('N', 2), ('N', 3), ('S', 6), ('S', 7), ('F', 2), ('F', 3), ('N', 4),
    ('N', 5), ('F', 4), ('F', 5), ('N', 6), ('N', 7), ('F', 6), ('F', 7), ('t', 0),
    ('s', 0), ('n', 0), ('s', 1), ('y', 0, 1), ('n', 1), ('f', 0), ('xn', 0), ('s', 2),
    ('y', 1, 1), ('y', 0, 2), ('f', 1), ('xn', 1), ('xf', 0), ('en', 0), ('s', 3), ('y', 2, 1),
    ('y', 1, 2), ('y', 0, 3), ('n', 2), ('n', 3), ('xf', 1), ('en', 1), ('ef', 0), ('s', 4),
    ('y', 3, 1), ('y', 2, 2), ('y', 1, 3), ('f', 2), ('f', 3), ('xn', 2), ('xn', 3), ('e', 0),
    ('ef', 1), ('mn', 0), ('s', 5), ('y', 4, 1), ('y', 3, 2), ('y', 2, 3), ('n', 4), ('n', 5),
    ('xf', 2), ('xf', 3), ('e', 1), ('en', 2), ('en', 3), ('mn', 1), ('s', 6), ('y', 5, 1),
    ('y', 4, 2), ('y', 3, 3), ('f', 4), ('f', 5), ('xn', 4), ('xn', 5), ('e', 2), ('ef', 2),
    ('ef', 3), ('mn', 2), ('s', 7), ('y', 6, 1), ('y', 5, 2), ('y', 4, 3), ('n', 6), ('n', 7),
    ('xf', 4), ('xf', 5), ('e', 3), ('en', 4), ('en', 5), ('mn', 3), ('y', 7, 1), ('y', 6, 2),
    ('y', 5, 3), ('f', 6), ('f', 7), ('xn', 6), ('xn', 7), ('e', 4), ('ef', 4), ('ef', 5),
    ('mn', 4), ('mf', 0), ('mf', 4), ('mf', 5), ('y', 7, 2), ('y', 6, 3), ('xf', 6), ('xf', 7),
    ('e', 5), ('en', 6), ('en', 7), ('mn', 5), ('mf', 1), ('y', 7, 3), ('e', 6), ('ef', 6),
    ('ef', 7), ('mn', 6), ('mf', 2), ('mf', 6), ('mf', 7), ('e', 7), ('mn', 7), ('mf', 3),
)
MESH = pl.DeviceIdType.MESH


def kernel(
    s_ref, r_ref, so_ref, ro_ref, si_ref, ri_ref, out_ref,
    a_buf, b_buf, acc, taper, ints, a_sem, b_sem, z_sem, yr_sem, yl_sem, xr_sem, xl_sem, i_sem,
):
    shot = lax.axis_index("shot")
    y = lax.axis_index("recv")
    u = lax.axis_index("surf")
    zh, x = shot // 4, shot % 4
    zl, c = u // 2, u % 2
    rows = s_ref.shape[2]
    cols = s_ref.shape[3]
    half = 4 * rows

    def turn(b):
        if b == 1:
            return zl + 1 - 2 * (zl % 2)
        return 3 - zl if b == 3 else (zl + b) % 4

    def surf_of(step):
        b, e = step
        return turn(b) * 2 + (c + e) % 2

    dest_of = surf_of

    def a_at(v, origin):
        return a_buf.at[v, :, pl.ds(pl.multiple_of(origin * rows, rows), rows), :]

    def b_at(v, origin):
        return b_buf.at[v, :, pl.ds(pl.multiple_of(origin * rows, rows), rows), :]

    def s_of(h, xx):
        return h * 4 + xx

    right = {"recv": (y + 1) % 8}
    left = {"recv": (y + 7) % 8}
    xright = {"shot": s_of(zh, (x + 1) % 4)}
    xleft = {"shot": s_of(zh, (x + 3) % 4)}
    other = s_of(1 - zh, x)

    tables = (so_ref, ro_ref, si_ref, ri_ref)
    for i, table in enumerate(tables):
        pltpu.make_async_copy(table, ints.at[i], i_sem.at[i]).start()
    pltpu.make_async_copy(s_ref.at[u], a_at(u, y), a_sem.at[u, y]).start()
    pltpu.make_async_copy(r_ref.at[u], b_at(u, shot), b_sem.at[u, shot]).start()

    barrier = pltpu.get_barrier_semaphore()
    peers = [right, left, xright, xleft]
    for step in NEAR:
        f = dest_of(step)
        if step != (0, 0):
            peers.append({"surf": f})
        peers.append({"shot": other, "surf": f})
    for peer in peers:
        pl.semaphore_signal(barrier, inc=1, device_id=peer, device_id_type=MESH)
    pl.semaphore_wait(barrier, len(peers))

    started = []

    def send(src, dst, send_sem, recv_sem, device):
        copy = pltpu.make_async_remote_copy(
            src_ref=src, dst_ref=dst, send_sem=send_sem, recv_sem=recv_sem, device_id=device, device_id_type=MESH
        )
        copy.start()
        started.append(copy)

    def a_wait(v, origin):
        pltpu.make_async_copy(a_at(v, origin), a_at(v, origin), a_sem.at[v, origin]).wait()

    def b_wait(v, origin):
        pltpu.make_async_copy(b_at(v, origin), b_at(v, origin), b_sem.at[v, origin]).wait()

    def a_right(v, origin):
        send(a_at(v, origin), a_at(v, origin), yr_sem.at[v, origin], a_sem.at[v, origin], right)

    def a_left(v, origin):
        send(a_at(v, origin), a_at(v, origin), yl_sem.at[v, origin], a_sem.at[v, origin], left)

    def b_right(v, origin):
        send(b_at(v, origin), b_at(v, origin), xr_sem.at[v, origin], b_sem.at[v, origin], xright)

    def b_left(v, origin):
        send(b_at(v, origin), b_at(v, origin), xl_sem.at[v, origin], b_sem.at[v, origin], xleft)

    def dot(v, h, ca, cb):
        here = pl.ds(pl.multiple_of(h * half, half), half)
        return lax.dot_general(
            a_buf[v, ca, here, :], b_buf[v, cb, here, :], (((0,), (0,)), ((), ())), preferred_element_type=jnp.float32
        )

    def multiply(v, h):
        acc[0] += dot(v, h, 0, 0) - dot(v, h, 1, 1)
        acc[1] += dot(v, h, 0, 1) + dot(v, h, 1, 0)

    def prepare():
        acc[...] = jnp.zeros_like(acc)
        for i, table in enumerate(tables):
            pltpu.make_async_copy(table, ints.at[i], i_sem.at[i]).wait()

        def rows_of(i):
            return jnp.broadcast_to(ints[pl.ds(i, 1), :].astype(jnp.float32), (cols, cols))

        lane = lax.broadcasted_iota(jnp.int32, (cols, cols), 1)
        shot_pos = (rows_of(0) + (lane + shot * cols).astype(jnp.float32)).T
        recv_pos = rows_of(1) + (lane + y * cols).astype(jnp.float32)
        distance = jnp.abs(recv_pos - shot_pos)
        width = 256.0 * (2.0 + rows_of(2).T + rows_of(3))
        taper[...] = 0.5 * (1.0 + jnp.cos(jnp.pi * (jnp.minimum(distance, width) / width)))

    def run(op):
        kind, i = op[0], op[1]
        if kind == "S" and i > 0:
            f = dest_of(NEAR[i])
            send(s_ref.at[f], a_at(u, y), z_sem.at[0, i], a_sem.at[u, y], {"surf": f})
        elif kind == "N" and i > 0:
            f = dest_of(NEAR[i])
            send(r_ref.at[f], b_at(u, shot), z_sem.at[1, i], b_sem.at[u, shot], {"surf": f})
        elif kind == "F":
            f = dest_of(FAR[i])
            send(r_ref.at[f], b_at(u, shot), z_sem.at[2, i], b_sem.at[u, shot], {"shot": other, "surf": f})
        elif kind == "s":
            v = surf_of(NEAR[i])
            a_wait(v, y)
            a_right(v, y)
            a_left(v, y)
        elif kind == "y":
            lag = op[2]
            v = surf_of(NEAR[i])
            before, after = (y + 8 - lag) % 8, (y + lag) % 8
            a_wait(v, before)
            if lag < 3 or i % 2 == 0:
                a_right(v, before)
            a_wait(v, after)
            if lag < 3 or i % 2 == 1:
                a_left(v, after)
        elif kind == "e":
            a_wait(surf_of(NEAR[i]), (y + 4) % 8)
        elif kind in ("n", "f"):
            v = surf_of((NEAR if kind == "n" else FAR)[i])
            origin = shot if kind == "n" else other
            b_wait(v, origin)
            b_right(v, origin)
            b_left(v, origin)
        elif kind in ("xn", "xf", "en", "ef"):
            near = kind[1] == "n"
            v = surf_of((NEAR if near else FAR)[i])
            h = zh if near else 1 - zh
            flip = (i % 2 == 1) == near
            if kind[0] == "x":
                if flip:
                    b_wait(v, s_of(h, (x + 1) % 4))
                    b_left(v, s_of(h, (x + 1) % 4))
                else:
                    b_wait(v, s_of(h, (x + 3) % 4))
                    b_right(v, s_of(h, (x + 3) % 4))
            else:
                b_wait(v, s_of(h, (x + 3) % 4) if flip else s_of(h, (x + 1) % 4))
                b_wait(v, s_of(h, (x + 2) % 4))
        elif kind == "mn":
            multiply(surf_of(NEAR[i]), zh)
        elif kind == "mf":
            multiply(surf_of(FAR[i]), 1 - zh)
        elif kind == "t":
            prepare()

    for op in PROGRAM:
        run(op)
    out_ref[...] = acc[...] * taper[...][None]
    for copy in started:
        copy.wait_send()


def predict(*args):
    freqs, parts, rows, cols = args[0].shape
    dma = pltpu.SemaphoreType.DMA
    return pl.pallas_call(
        kernel,
        out_shape=jax.ShapeDtypeStruct((parts, cols, cols), jnp.float32),
        in_specs=[pl.BlockSpec(memory_space=pl.ANY)] * 6,
        out_specs=pl.BlockSpec(memory_space=pltpu.VMEM),
        scratch_shapes=[
            pltpu.VMEM((freqs, parts, 8 * rows, cols), args[0].dtype),
            pltpu.VMEM((freqs, parts, 8 * rows, cols), args[0].dtype),
            pltpu.VMEM((parts, cols, cols), jnp.float32),
            pltpu.VMEM((cols, cols), jnp.float32),
            pltpu.VMEM((4, cols), jnp.int32),
            dma((8, 8)),
            dma((8, 8)),
            dma((3, 8)),
            dma((8, 8)),
            dma((8, 8)),
            dma((8, 8)),
            dma((8, 8)),
            dma((4,)),
        ],
        compiler_params=pltpu.CompilerParams(
            collective_id=0, has_side_effects=True, vmem_limit_bytes=60 * 1024 * 1024
        ),
    )(*args)


def solution(mesh):
    placed = (
        P(None, None, ("surf", "recv"), "shot"),
        P(None, None, ("surf", "shot"), "recv"),
        P("shot"),
        P("recv"),
        P("shot"),
        P("recv"),
    )
    return jax.shard_map(
        lambda *args: predict(*args)[None],
        mesh=mesh,
        in_specs=placed,
        out_specs=P("surf", None, "shot", "recv"),
        check_vma=False,
    )
```

```python
import jax
import jax.numpy as jnp
from jax import lax
from jax.experimental import pallas as pl
from jax.experimental.pallas import tpu as pltpu
from jax.sharding import PartitionSpec as P

NEAR = ((0, 0), (0, 1), (1, 0), (1, 1), (2, 0), (2, 1), (3, 0), (3, 1))
FAR = ((2, 0), (2, 1), (3, 0), (3, 1), (1, 0), (1, 1), (0, 0), (0, 1))
PROGRAM = (
    ('S', 1), ('N', 1), ('S', 2), ('S', 3), ('F', 0), ('F', 1), ('N', 2), ('N', 3),
    ('S', 4), ('S', 5), ('F', 2), ('F', 3), ('S', 6), ('S', 7), ('N', 4), ('N', 5),
    ('F', 4), ('F', 5), ('N', 6), ('N', 7), ('F', 6), ('F', 7), ('s', 0), ('n', 0),
    ('s', 1), ('y', 0, 1), ('n', 1), ('xn', 0), ('s', 2), ('y', 1, 1), ('y', 0, 2), ('f', 0),
    ('f', 1), ('xn', 1), ('en', 0), ('s', 3), ('y', 2, 1), ('y', 1, 2), ('y', 0, 3), ('n', 2),
    ('n', 3), ('xf', 0), ('xf', 1), ('en', 1), ('s', 4), ('y', 3, 1), ('y', 2, 2), ('y', 1, 3),
    ('f', 2), ('f', 3), ('xn', 2), ('xn', 3), ('e', 0), ('ef', 0), ('ef', 1), ('mn', 0),
    ('s', 5), ('y', 4, 1), ('y', 3, 2), ('y', 2, 3), ('n', 4), ('n', 5), ('xf', 2), ('xf', 3),
    ('e', 1), ('en', 2), ('en', 3), ('mn', 1), ('s', 6), ('y', 5, 1), ('y', 4, 2), ('y', 3, 3),
    ('f', 4), ('f', 5), ('xn', 4), ('xn', 5), ('e', 2), ('ef', 2), ('ef', 3), ('mn', 2),
    ('s', 7), ('y', 6, 1), ('y', 5, 2), ('y', 4, 3), ('n', 6), ('n', 7), ('xf', 4), ('xf', 5),
    ('e', 3), ('en', 4), ('en', 5), ('mn', 3), ('y', 7, 1), ('y', 6, 2), ('y', 5, 3), ('f', 6),
    ('f', 7), ('xn', 6), ('xn', 7), ('e', 4), ('ef', 4), ('ef', 5), ('mn', 4), ('mf', 0),
    ('mf', 4), ('mf', 5), ('y', 7, 2), ('y', 6, 3), ('xf', 6), ('xf', 7), ('e', 5), ('en', 6),
    ('en', 7), ('mn', 5), ('mf', 1), ('y', 7, 3), ('e', 6), ('ef', 6), ('ef', 7), ('mn', 6),
    ('mf', 2), ('mf', 6), ('mf', 7), ('e', 7), ('mn', 7), ('mf', 3),
)
MESH = pl.DeviceIdType.MESH


def kernel(
    s_ref, r_ref, so_ref, ro_ref, si_ref, ri_ref, out_ref,
    a_buf, b_buf, acc, taper, ints, a_sem, b_sem, z_sem, yr_sem, yl_sem, xr_sem, xl_sem, i_sem,
):
    shot = lax.axis_index("shot")
    y = lax.axis_index("recv")
    u = lax.axis_index("surf")
    zh, x = shot // 4, shot % 4
    zl, c = u // 2, u % 2
    rows = s_ref.shape[2]
    cols = s_ref.shape[3]
    half = 4 * rows

    def turn(b):
        if b == 1:
            return zl + 1 - 2 * (zl % 2)
        return 3 - zl if b == 3 else (zl + b) % 4

    def surf_of(step):
        b, e = step
        return turn(b) * 2 + (c + e) % 2

    dest_of = surf_of

    def a_at(v, origin):
        return a_buf.at[v, :, pl.ds(pl.multiple_of(origin * rows, rows), rows), :]

    def b_at(v, origin):
        return b_buf.at[v, :, pl.ds(pl.multiple_of(origin * rows, rows), rows), :]

    def s_of(h, xx):
        return h * 4 + xx

    right = {"recv": (y + 1) % 8}
    left = {"recv": (y + 7) % 8}
    xright = {"shot": s_of(zh, (x + 1) % 4)}
    xleft = {"shot": s_of(zh, (x + 3) % 4)}
    other = s_of(1 - zh, x)

    tables = (so_ref, ro_ref, si_ref, ri_ref)
    for i, table in enumerate(tables):
        pltpu.make_async_copy(table, ints.at[i], i_sem.at[i]).start()
    pltpu.make_async_copy(s_ref.at[u], a_at(u, y), a_sem.at[u, y]).start()
    pltpu.make_async_copy(r_ref.at[u], b_at(u, shot), b_sem.at[u, shot]).start()

    barrier = pltpu.get_barrier_semaphore()
    peers = [{"shot": other, "surf": dest_of(step)} for step in NEAR]
    peers += [{"surf": dest_of(step)} for step in NEAR[:0:-1]]
    peers += [right, left, xright, xleft]
    for peer in peers:
        pl.semaphore_signal(barrier, inc=1, device_id=peer, device_id_type=MESH)

    started = []

    def send(src, dst, send_sem, recv_sem, device):
        copy = pltpu.make_async_remote_copy(
            src_ref=src, dst_ref=dst, send_sem=send_sem, recv_sem=recv_sem, device_id=device, device_id_type=MESH
        )
        copy.start()
        started.append(copy)

    def a_wait(v, origin):
        pltpu.make_async_copy(a_at(v, origin), a_at(v, origin), a_sem.at[v, origin]).wait()

    def b_wait(v, origin):
        pltpu.make_async_copy(b_at(v, origin), b_at(v, origin), b_sem.at[v, origin]).wait()

    def a_right(v, origin):
        send(a_at(v, origin), a_at(v, origin), yr_sem.at[v, origin], a_sem.at[v, origin], right)

    def a_left(v, origin):
        send(a_at(v, origin), a_at(v, origin), yl_sem.at[v, origin], a_sem.at[v, origin], left)

    def b_right(v, origin):
        send(b_at(v, origin), b_at(v, origin), xr_sem.at[v, origin], b_sem.at[v, origin], xright)

    def b_left(v, origin):
        send(b_at(v, origin), b_at(v, origin), xl_sem.at[v, origin], b_sem.at[v, origin], xleft)

    def dot(v, h, ca, cb):
        here = pl.ds(pl.multiple_of(h * half, half), half)
        return lax.dot_general(
            a_buf[v, ca, here, :], b_buf[v, cb, here, :], (((0,), (0,)), ((), ())), preferred_element_type=jnp.float32
        )

    def multiply(v, h):
        acc[0] += dot(v, h, 0, 0) - dot(v, h, 1, 1)
        acc[1] += dot(v, h, 0, 1) + dot(v, h, 1, 0)

    def prepare():
        acc[...] = jnp.zeros_like(acc)
        for i, table in enumerate(tables):
            pltpu.make_async_copy(table, ints.at[i], i_sem.at[i]).wait()

        def rows_of(i):
            return jnp.broadcast_to(ints[pl.ds(i, 1), :].astype(jnp.float32), (cols, cols))

        lane = lax.broadcasted_iota(jnp.int32, (cols, cols), 1)
        shot_pos = (rows_of(0) + (lane + shot * cols).astype(jnp.float32)).T
        recv_pos = rows_of(1) + (lane + y * cols).astype(jnp.float32)
        distance = jnp.abs(recv_pos - shot_pos)
        width = 256.0 * (2.0 + rows_of(2).T + rows_of(3))
        taper[...] = 0.5 * (1.0 + jnp.cos(jnp.pi * (jnp.minimum(distance, width) / width)))

    def run(op):
        kind, i = op[0], op[1]
        if kind == "S" and i > 0:
            f = dest_of(NEAR[i])
            send(s_ref.at[f], a_at(u, y), z_sem.at[0, i], a_sem.at[u, y], {"surf": f})
        elif kind == "N" and i > 0:
            f = dest_of(NEAR[i])
            send(r_ref.at[f], b_at(u, shot), z_sem.at[1, i], b_sem.at[u, shot], {"surf": f})
        elif kind == "F":
            f = dest_of(FAR[i])
            send(r_ref.at[f], b_at(u, shot), z_sem.at[2, i], b_sem.at[u, shot], {"shot": other, "surf": f})
        elif kind == "s":
            v = surf_of(NEAR[i])
            a_wait(v, y)
            a_right(v, y)
            a_left(v, y)
        elif kind == "y":
            lag = op[2]
            v = surf_of(NEAR[i])
            before, after = (y + 8 - lag) % 8, (y + lag) % 8
            a_wait(v, before)
            if lag < 3 or i % 2 == 0:
                a_right(v, before)
            a_wait(v, after)
            if lag < 3 or i % 2 == 1:
                a_left(v, after)
        elif kind == "e":
            a_wait(surf_of(NEAR[i]), (y + 4) % 8)
        elif kind in ("n", "f"):
            v = surf_of((NEAR if kind == "n" else FAR)[i])
            origin = shot if kind == "n" else other
            b_wait(v, origin)
            b_right(v, origin)
            b_left(v, origin)
        elif kind in ("xn", "xf", "en", "ef"):
            near = kind[1] == "n"
            v = surf_of((NEAR if near else FAR)[i])
            h = zh if near else 1 - zh
            flip = (i % 2 == 1) == near
            if kind[0] == "x":
                if flip:
                    b_wait(v, s_of(h, (x + 1) % 4))
                    b_left(v, s_of(h, (x + 1) % 4))
                else:
                    b_wait(v, s_of(h, (x + 3) % 4))
                    b_right(v, s_of(h, (x + 3) % 4))
            else:
                b_wait(v, s_of(h, (x + 3) % 4) if flip else s_of(h, (x + 1) % 4))
                b_wait(v, s_of(h, (x + 2) % 4))
        elif kind == "mn":
            multiply(surf_of(NEAR[i]), zh)
        elif kind == "mf":
            multiply(surf_of(FAR[i]), 1 - zh)

    prepare()
    pl.semaphore_wait(barrier, len(peers))
    for op in PROGRAM:
        run(op)
    out_ref[...] = acc[...] * taper[...][None]
    for copy in started:
        copy.wait_send()


def predict(*args):
    freqs, parts, rows, cols = args[0].shape
    dma = pltpu.SemaphoreType.DMA
    return pl.pallas_call(
        kernel,
        out_shape=jax.ShapeDtypeStruct((parts, cols, cols), jnp.float32),
        in_specs=[pl.BlockSpec(memory_space=pl.ANY)] * 6,
        out_specs=pl.BlockSpec(memory_space=pltpu.VMEM),
        scratch_shapes=[
            pltpu.VMEM((freqs, parts, 8 * rows, cols), args[0].dtype),
            pltpu.VMEM((freqs, parts, 8 * rows, cols), args[0].dtype),
            pltpu.VMEM((parts, cols, cols), jnp.float32),
            pltpu.VMEM((cols, cols), jnp.float32),
            pltpu.VMEM((4, cols), jnp.int32),
            dma((8, 8)),
            dma((8, 8)),
            dma((3, 8)),
            dma((8, 8)),
            dma((8, 8)),
            dma((8, 8)),
            dma((8, 8)),
            dma((4,)),
        ],
        compiler_params=pltpu.CompilerParams(
            collective_id=0, has_side_effects=True, vmem_limit_bytes=40 * 1024 * 1024
        ),
    )(*(pltpu.with_memory_space_constraint(a, pltpu.HBM) for a in args))


def solution(mesh):
    placed = (
        P(None, None, ("surf", "recv"), "shot"),
        P(None, None, ("surf", "shot"), "recv"),
        P("shot"),
        P("recv"),
        P("shot"),
        P("recv"),
    )
    return jax.shard_map(
        lambda *args: predict(*args)[None],
        mesh=mesh,
        in_specs=placed,
        out_specs=P("surf", None, "shot", "recv"),
        check_vma=False,
    )
```

```python
import functools

import jax
import jax.numpy as jnp
from jax import lax
from jax.experimental import pallas as pl
from jax.experimental.pallas import tpu as pltpu
from jax.sharding import PartitionSpec as P

NEAR = ((0, 0), (0, 1), (1, 0), (1, 1), (2, 0), (2, 1), (3, 0), (3, 1))
FAR = ((2, 0), (2, 1), (3, 0), (3, 1), (1, 0), (1, 1), (0, 0), (0, 1))
PROGRAM = (
    ('S', 1), ('N', 1), ('S', 2), ('S', 3), ('F', 0), ('F', 1), ('N', 2), ('N', 3),
    ('S', 4), ('S', 5), ('F', 2), ('F', 3), ('N', 4), ('N', 5), ('S', 6), ('S', 7),
    ('F', 4), ('F', 5), ('N', 6), ('N', 7), ('F', 6), ('F', 7), ('s', 0), ('n', 0),
    ('s', 1), ('y', 0, 1), ('n', 1), ('xn', 0), ('s', 2), ('y', 1, 1), ('y', 0, 2), ('f', 0),
    ('f', 1), ('xn', 1), ('en', 0), ('s', 3), ('y', 2, 1), ('y', 1, 2), ('y', 0, 3), ('n', 2),
    ('n', 3), ('xf', 0), ('xf', 1), ('en', 1), ('s', 4), ('y', 3, 1), ('y', 2, 2), ('y', 1, 3),
    ('f', 2), ('f', 3), ('xn', 2), ('xn', 3), ('e', 0), ('ef', 0), ('ef', 1), ('mn', 0),
    ('s', 5), ('y', 4, 1), ('y', 3, 2), ('y', 2, 3), ('n', 4), ('n', 5), ('xf', 2), ('xf', 3),
    ('e', 1), ('en', 2), ('en', 3), ('mn', 1), ('s', 6), ('y', 5, 1), ('y', 4, 2), ('y', 3, 3),
    ('f', 4), ('f', 5), ('xn', 4), ('xn', 5), ('e', 2), ('ef', 2), ('ef', 3), ('mn', 2),
    ('s', 7), ('y', 6, 1), ('y', 5, 2), ('y', 4, 3), ('n', 6), ('n', 7), ('xf', 4), ('xf', 5),
    ('e', 3), ('en', 4), ('en', 5), ('mn', 3), ('y', 7, 1), ('y', 6, 2), ('y', 5, 3), ('f', 6),
    ('f', 7), ('xn', 6), ('xn', 7), ('e', 4), ('ef', 4), ('ef', 5), ('mn', 4), ('mf', 0),
    ('mf', 4), ('mf', 5), ('y', 7, 2), ('y', 6, 3), ('xf', 6), ('xf', 7), ('e', 5), ('en', 6),
    ('en', 7), ('mn', 5), ('mf', 1), ('y', 7, 3), ('e', 6), ('ef', 6), ('ef', 7), ('mn', 6),
    ('mf', 2), ('mf', 6), ('mf', 7), ('e', 7), ('mn', 7), ('mf', 3),
)
MESH = pl.DeviceIdType.MESH


def kernel(
    s_ref, r_ref, so_ref, ro_ref, si_ref, ri_ref, out_ref,
    a_buf, b_buf, acc, taper, ints, a_sem, b_sem, z_sem, yr_sem, yl_sem, xr_sem, xl_sem, i_sem,
):
    shot = lax.axis_index("shot")
    y = lax.axis_index("recv")
    u = lax.axis_index("surf")
    zh, x = shot // 4, shot % 4
    zl, c = u // 2, u % 2
    rows = s_ref.shape[2]
    cols = s_ref.shape[3]
    half = 4 * rows

    def turn(b):
        if b == 1:
            return zl + 1 - 2 * (zl % 2)
        return 3 - zl if b == 3 else (zl + b) % 4

    def surf_of(step):
        b, e = step
        return turn(b) * 2 + (c + e) % 2

    dest_of = surf_of

    def a_at(v, origin):
        return a_buf.at[v, :, pl.ds(pl.multiple_of(origin * rows, rows), rows), :]

    def b_at(v, origin):
        return b_buf.at[v, :, pl.ds(pl.multiple_of(origin * rows, rows), rows), :]

    def s_of(h, xx):
        return h * 4 + xx

    right = {"recv": (y + 1) % 8}
    left = {"recv": (y + 7) % 8}
    xright = {"shot": s_of(zh, (x + 1) % 4)}
    xleft = {"shot": s_of(zh, (x + 3) % 4)}
    other = s_of(1 - zh, x)

    tables = (so_ref, ro_ref, si_ref, ri_ref)
    for i, table in enumerate(tables):
        pltpu.make_async_copy(table, ints.at[i], i_sem.at[i]).start()
    pltpu.make_async_copy(s_ref.at[u], a_at(u, y), a_sem.at[u, y]).start()
    pltpu.make_async_copy(r_ref.at[u], b_at(u, shot), b_sem.at[u, shot]).start()

    barrier = pltpu.get_barrier_semaphore()
    peers = [{"shot": other, "surf": dest_of(step)} for step in NEAR]
    peers += [{"surf": dest_of(step)} for step in NEAR[:0:-1]]
    peers += [right, left, xright, xleft]
    for peer in peers:
        pl.semaphore_signal(barrier, inc=1, device_id=peer, device_id_type=MESH)

    started = []

    def send(src, dst, send_sem, recv_sem, device):
        copy = pltpu.make_async_remote_copy(
            src_ref=src, dst_ref=dst, send_sem=send_sem, recv_sem=recv_sem, device_id=device, device_id_type=MESH
        )
        copy.start()
        started.append(copy)

    def a_wait(v, origin):
        pltpu.make_async_copy(a_at(v, origin), a_at(v, origin), a_sem.at[v, origin]).wait()

    def b_wait(v, origin):
        pltpu.make_async_copy(b_at(v, origin), b_at(v, origin), b_sem.at[v, origin]).wait()

    def a_right(v, origin):
        send(a_at(v, origin), a_at(v, origin), yr_sem.at[v, origin], a_sem.at[v, origin], right)

    def a_left(v, origin):
        send(a_at(v, origin), a_at(v, origin), yl_sem.at[v, origin], a_sem.at[v, origin], left)

    def b_right(v, origin):
        send(b_at(v, origin), b_at(v, origin), xr_sem.at[v, origin], b_sem.at[v, origin], xright)

    def b_left(v, origin):
        send(b_at(v, origin), b_at(v, origin), xl_sem.at[v, origin], b_sem.at[v, origin], xleft)

    def multiply(v, h):
        here = pl.ds(pl.multiple_of(h * half, half), half)
        left_re, left_im = a_buf[v, 0, here, :].T, a_buf[v, 1, here, :].T
        right_re, right_im = b_buf[v, 0, here, :], b_buf[v, 1, here, :]
        dot = functools.partial(jnp.dot, preferred_element_type=jnp.float32)
        acc[0] += dot(left_re, right_re) - dot(left_im, right_im)
        acc[1] += dot(left_re, right_im) + dot(left_im, right_re)

    def prepare():
        acc[...] = jnp.zeros_like(acc)
        for i, table in enumerate(tables):
            pltpu.make_async_copy(table, ints.at[i], i_sem.at[i]).wait()

        def rows_of(i):
            return jnp.broadcast_to(ints[pl.ds(i, 1), :].astype(jnp.float32), (cols, cols))

        lane = lax.broadcasted_iota(jnp.int32, (cols, cols), 1)
        shot_pos = (rows_of(0) + (lane + shot * cols).astype(jnp.float32)).T
        recv_pos = rows_of(1) + (lane + y * cols).astype(jnp.float32)
        distance = jnp.abs(recv_pos - shot_pos)
        width = 256.0 * (2.0 + rows_of(2).T + rows_of(3))
        taper[...] = 0.5 * (1.0 + jnp.cos(jnp.pi * (jnp.minimum(distance, width) / width)))

    def run(op):
        kind, i = op[0], op[1]
        if kind == "S" and i > 0:
            f = dest_of(NEAR[i])
            send(s_ref.at[f], a_at(u, y), z_sem.at[0, i], a_sem.at[u, y], {"surf": f})
        elif kind == "N" and i > 0:
            f = dest_of(NEAR[i])
            send(r_ref.at[f], b_at(u, shot), z_sem.at[1, i], b_sem.at[u, shot], {"surf": f})
        elif kind == "F":
            f = dest_of(FAR[i])
            send(r_ref.at[f], b_at(u, shot), z_sem.at[2, i], b_sem.at[u, shot], {"shot": other, "surf": f})
        elif kind == "s":
            v = surf_of(NEAR[i])
            a_wait(v, y)
            a_right(v, y)
            a_left(v, y)
        elif kind == "y":
            lag = op[2]
            v = surf_of(NEAR[i])
            before, after = (y + 8 - lag) % 8, (y + lag) % 8
            a_wait(v, before)
            if lag < 3 or i % 2 == 0:
                a_right(v, before)
            a_wait(v, after)
            if lag < 3 or i % 2 == 1:
                a_left(v, after)
        elif kind == "e":
            a_wait(surf_of(NEAR[i]), (y + 4) % 8)
        elif kind in ("n", "f"):
            v = surf_of((NEAR if kind == "n" else FAR)[i])
            origin = shot if kind == "n" else other
            b_wait(v, origin)
            b_right(v, origin)
            b_left(v, origin)
        elif kind in ("xn", "xf", "en", "ef"):
            near = kind[1] == "n"
            v = surf_of((NEAR if near else FAR)[i])
            h = zh if near else 1 - zh
            flip = (i % 2 == 1) == near
            if kind[0] == "x":
                if flip:
                    b_wait(v, s_of(h, (x + 1) % 4))
                    b_left(v, s_of(h, (x + 1) % 4))
                else:
                    b_wait(v, s_of(h, (x + 3) % 4))
                    b_right(v, s_of(h, (x + 3) % 4))
            else:
                b_wait(v, s_of(h, (x + 3) % 4) if flip else s_of(h, (x + 1) % 4))
                b_wait(v, s_of(h, (x + 2) % 4))
        elif kind == "mn":
            multiply(surf_of(NEAR[i]), zh)
        elif kind == "mf":
            multiply(surf_of(FAR[i]), 1 - zh)

    prepare()
    pl.semaphore_wait(barrier, len(peers))
    for op in PROGRAM:
        run(op)
    out_ref[...] = acc[...] * taper[...][None]
    for copy in started:
        copy.wait_send()


def predict(*args):
    freqs, parts, rows, cols = args[0].shape
    dma = pltpu.SemaphoreType.DMA
    return pl.pallas_call(
        kernel,
        out_shape=jax.ShapeDtypeStruct((parts, cols, cols), jnp.float32),
        in_specs=[pl.BlockSpec(memory_space=pl.ANY)] * 6,
        out_specs=pl.BlockSpec(memory_space=pltpu.VMEM),
        scratch_shapes=[
            pltpu.VMEM((freqs, parts, 8 * rows, cols), args[0].dtype),
            pltpu.VMEM((freqs, parts, 8 * rows, cols), args[0].dtype),
            pltpu.VMEM((parts, cols, cols), jnp.float32),
            pltpu.VMEM((cols, cols), jnp.float32),
            pltpu.VMEM((4, cols), jnp.int32),
            dma((8, 8)),
            dma((8, 8)),
            dma((3, 8)),
            dma((8, 8)),
            dma((8, 8)),
            dma((8, 8)),
            dma((8, 8)),
            dma((4,)),
        ],
        compiler_params=pltpu.CompilerParams(
            collective_id=0, has_side_effects=True, vmem_limit_bytes=40 * 1024 * 1024
        ),
    )(*(pltpu.with_memory_space_constraint(a, pltpu.HBM) for a in args))


def solution(mesh):
    placed = (
        P(None, None, ("surf", "recv"), "shot"),
        P(None, None, ("surf", "shot"), "recv"),
        P("shot"),
        P("recv"),
        P("shot"),
        P("recv"),
    )
    return jax.shard_map(
        lambda *args: predict(*args)[None],
        mesh=mesh,
        in_specs=placed,
        out_specs=P("surf", None, "shot", "recv"),
        check_vma=False,
    )
```

```python
import functools

import jax
import jax.numpy as jnp
from jax import lax
from jax.experimental import pallas as pl
from jax.experimental.pallas import tpu as pltpu
from jax.sharding import PartitionSpec as P

NEAR = ((0, 0), (0, 1), (1, 0), (1, 1), (2, 0), (2, 1), (3, 0), (3, 1))
FAR = ((2, 0), (2, 1), (3, 0), (3, 1), (1, 0), (1, 1), (0, 0), (0, 1))
PROGRAM = (
    ('S', 1), ('N', 1), ('S', 2), ('S', 3), ('F', 0), ('F', 1), ('N', 2), ('N', 3),
    ('S', 4), ('S', 5), ('F', 2), ('F', 3), ('N', 4), ('N', 5), ('S', 6), ('S', 7),
    ('F', 4), ('F', 5), ('N', 6), ('N', 7), ('F', 6), ('F', 7), ('s', 0), ('n', 0),
    ('s', 1), ('y', 0, 1), ('n', 1), ('xn', 0), ('s', 2), ('y', 1, 1), ('y', 0, 2), ('f', 0),
    ('f', 1), ('xn', 1), ('en', 0), ('s', 3), ('y', 2, 1), ('y', 1, 2), ('y', 0, 3), ('n', 2),
    ('n', 3), ('xf', 0), ('xf', 1), ('en', 1), ('s', 4), ('y', 3, 1), ('y', 2, 2), ('y', 1, 3),
    ('f', 2), ('f', 3), ('xn', 2), ('xn', 3), ('e', 0), ('ef', 0), ('ef', 1), ('mn', 0),
    ('s', 5), ('y', 4, 1), ('y', 3, 2), ('y', 2, 3), ('n', 4), ('n', 5), ('xf', 2), ('xf', 3),
    ('e', 1), ('en', 2), ('en', 3), ('mn', 1), ('s', 6), ('y', 5, 1), ('y', 4, 2), ('y', 3, 3),
    ('f', 4), ('f', 5), ('xn', 4), ('xn', 5), ('e', 2), ('ef', 2), ('ef', 3), ('mn', 2),
    ('s', 7), ('y', 6, 1), ('y', 5, 2), ('y', 4, 3), ('n', 6), ('n', 7), ('xf', 4), ('xf', 5),
    ('e', 3), ('en', 4), ('en', 5), ('mn', 3), ('y', 7, 1), ('y', 6, 2), ('y', 5, 3), ('f', 6),
    ('f', 7), ('xn', 6), ('xn', 7), ('e', 4), ('ef', 4), ('ef', 5), ('mn', 4), ('mf', 0),
    ('mf', 4), ('mf', 5), ('y', 7, 2), ('y', 6, 3), ('xf', 6), ('xf', 7), ('e', 5), ('en', 6),
    ('en', 7), ('mn', 5), ('mf', 1), ('y', 7, 3), ('e', 6), ('ef', 6), ('ef', 7),
    ('mw', 6), ('mf', 6), ('mf', 7), ('e', 7),  ('mw', 7),
)
MESH = pl.DeviceIdType.MESH


def kernel(
    s_ref, r_ref, so_ref, ro_ref, si_ref, ri_ref, out_ref,
    a_buf, b_buf, acc, taper, ints, a_sem, b_sem, z_sem, yr_sem, yl_sem, xr_sem, xl_sem, i_sem,
):
    shot = lax.axis_index("shot")
    y = lax.axis_index("recv")
    u = lax.axis_index("surf")
    zh, x = shot // 4, shot % 4
    zl, c = u // 2, u % 2
    rows = s_ref.shape[2]
    cols = s_ref.shape[3]
    half = 4 * rows

    def turn(b):
        if b == 1:
            return zl + 1 - 2 * (zl % 2)
        return 3 - zl if b == 3 else (zl + b) % 4

    def surf_of(step):
        b, e = step
        return turn(b) * 2 + (c + e) % 2

    dest_of = surf_of

    def a_at(v, origin):
        return a_buf.at[v, :, pl.ds(pl.multiple_of(origin * rows, rows), rows), :]

    def b_at(v, origin):
        return b_buf.at[v, :, pl.ds(pl.multiple_of(origin * rows, rows), rows), :]

    def s_of(h, xx):
        return h * 4 + xx

    right = {"recv": (y + 1) % 8}
    left = {"recv": (y + 7) % 8}
    xright = {"shot": s_of(zh, (x + 1) % 4)}
    xleft = {"shot": s_of(zh, (x + 3) % 4)}
    other = s_of(1 - zh, x)

    tables = (so_ref, ro_ref, si_ref, ri_ref)
    for i, table in enumerate(tables):
        pltpu.make_async_copy(table, ints.at[i], i_sem.at[i]).start()
    pltpu.make_async_copy(s_ref.at[u], a_at(u, y), a_sem.at[u, y]).start()
    pltpu.make_async_copy(r_ref.at[u], b_at(u, shot), b_sem.at[u, shot]).start()

    barrier = pltpu.get_barrier_semaphore()
    peers = [{"shot": other, "surf": dest_of(step)} for step in NEAR]
    peers += [{"surf": dest_of(step)} for step in NEAR[:0:-1]]
    peers += [right, left, xright, xleft]
    for peer in peers:
        pl.semaphore_signal(barrier, inc=1, device_id=peer, device_id_type=MESH)

    started = []

    def send(src, dst, send_sem, recv_sem, device):
        copy = pltpu.make_async_remote_copy(
            src_ref=src, dst_ref=dst, send_sem=send_sem, recv_sem=recv_sem, device_id=device, device_id_type=MESH
        )
        copy.start()
        started.append(copy)

    def a_wait(v, origin):
        pltpu.make_async_copy(a_at(v, origin), a_at(v, origin), a_sem.at[v, origin]).wait()

    def b_wait(v, origin):
        pltpu.make_async_copy(b_at(v, origin), b_at(v, origin), b_sem.at[v, origin]).wait()

    def a_right(v, origin):
        send(a_at(v, origin), a_at(v, origin), yr_sem.at[v, origin], a_sem.at[v, origin], right)

    def a_left(v, origin):
        send(a_at(v, origin), a_at(v, origin), yl_sem.at[v, origin], a_sem.at[v, origin], left)

    def b_right(v, origin):
        send(b_at(v, origin), b_at(v, origin), xr_sem.at[v, origin], b_sem.at[v, origin], xright)

    def b_left(v, origin):
        send(b_at(v, origin), b_at(v, origin), xl_sem.at[v, origin], b_sem.at[v, origin], xleft)

    def multiply(v, h):
        here = slice(None) if h is None else pl.ds(pl.multiple_of(h * half, half), half)
        left_re, left_im = a_buf[v, 0, here, :].T, a_buf[v, 1, here, :].T
        right_re, right_im = b_buf[v, 0, here, :], b_buf[v, 1, here, :]
        dot = functools.partial(jnp.dot, preferred_element_type=jnp.float32)
        acc[0] += dot(left_re, right_re) - dot(left_im, right_im)
        acc[1] += dot(left_re, right_im) + dot(left_im, right_re)

    def prepare():
        acc[...] = jnp.zeros_like(acc)
        for i, table in enumerate(tables):
            pltpu.make_async_copy(table, ints.at[i], i_sem.at[i]).wait()

        def rows_of(i):
            return jnp.broadcast_to(ints[pl.ds(i, 1), :].astype(jnp.float32), (cols, cols))

        lane = lax.broadcasted_iota(jnp.int32, (cols, cols), 1)
        shot_pos = (rows_of(0) + (lane + shot * cols).astype(jnp.float32)).T
        recv_pos = rows_of(1) + (lane + y * cols).astype(jnp.float32)
        distance = jnp.abs(recv_pos - shot_pos)
        width = 256.0 * (2.0 + rows_of(2).T + rows_of(3))
        taper[...] = 0.5 * (1.0 + jnp.cos(jnp.pi * (jnp.minimum(distance, width) / width)))

    def run(op):
        kind, i = op[0], op[1]
        if kind == "S" and i > 0:
            f = dest_of(NEAR[i])
            send(s_ref.at[f], a_at(u, y), z_sem.at[0, i], a_sem.at[u, y], {"surf": f})
        elif kind == "N" and i > 0:
            f = dest_of(NEAR[i])
            send(r_ref.at[f], b_at(u, shot), z_sem.at[1, i], b_sem.at[u, shot], {"surf": f})
        elif kind == "F":
            f = dest_of(FAR[i])
            send(r_ref.at[f], b_at(u, shot), z_sem.at[2, i], b_sem.at[u, shot], {"shot": other, "surf": f})
        elif kind == "s":
            v = surf_of(NEAR[i])
            a_wait(v, y)
            a_right(v, y)
            a_left(v, y)
        elif kind == "y":
            lag = op[2]
            v = surf_of(NEAR[i])
            before, after = (y + 8 - lag) % 8, (y + lag) % 8
            a_wait(v, before)
            if lag < 3 or i % 2 == 0:
                a_right(v, before)
            a_wait(v, after)
            if lag < 3 or i % 2 == 1:
                a_left(v, after)
        elif kind == "e":
            a_wait(surf_of(NEAR[i]), (y + 4) % 8)
        elif kind in ("n", "f"):
            v = surf_of((NEAR if kind == "n" else FAR)[i])
            origin = shot if kind == "n" else other
            b_wait(v, origin)
            b_right(v, origin)
            b_left(v, origin)
        elif kind in ("xn", "xf", "en", "ef"):
            near = kind[1] == "n"
            v = surf_of((NEAR if near else FAR)[i])
            h = zh if near else 1 - zh
            flip = (i % 2 == 1) == near
            if kind[0] == "x":
                if flip:
                    b_wait(v, s_of(h, (x + 1) % 4))
                    b_left(v, s_of(h, (x + 1) % 4))
                else:
                    b_wait(v, s_of(h, (x + 3) % 4))
                    b_right(v, s_of(h, (x + 3) % 4))
            else:
                b_wait(v, s_of(h, (x + 3) % 4) if flip else s_of(h, (x + 1) % 4))
                b_wait(v, s_of(h, (x + 2) % 4))
        elif kind == "mn":
            multiply(surf_of(NEAR[i]), zh)
        elif kind == "mw":
            multiply(surf_of(NEAR[i]), None)
        elif kind == "mf":
            multiply(surf_of(FAR[i]), 1 - zh)

    prepare()
    pl.semaphore_wait(barrier, len(peers))
    for op in PROGRAM:
        run(op)
    out_ref[...] = acc[...] * taper[...][None]
    for copy in started:
        copy.wait_send()


def predict(*args):
    freqs, parts, rows, cols = args[0].shape
    dma = pltpu.SemaphoreType.DMA
    return pl.pallas_call(
        kernel,
        out_shape=jax.ShapeDtypeStruct((parts, cols, cols), jnp.float32),
        in_specs=[pl.BlockSpec(memory_space=pl.ANY)] * 6,
        out_specs=pl.BlockSpec(memory_space=pltpu.VMEM),
        scratch_shapes=[
            pltpu.VMEM((freqs, parts, 8 * rows, cols), args[0].dtype),
            pltpu.VMEM((freqs, parts, 8 * rows, cols), args[0].dtype),
            pltpu.VMEM((parts, cols, cols), jnp.float32),
            pltpu.VMEM((cols, cols), jnp.float32),
            pltpu.VMEM((4, cols), jnp.int32),
            dma((8, 8)),
            dma((8, 8)),
            dma((3, 8)),
            dma((8, 8)),
            dma((8, 8)),
            dma((8, 8)),
            dma((8, 8)),
            dma((4,)),
        ],
        compiler_params=pltpu.CompilerParams(
            collective_id=0, has_side_effects=True, vmem_limit_bytes=40 * 1024 * 1024
        ),
    )(*(pltpu.with_memory_space_constraint(a, pltpu.HBM) for a in args))


def solution(mesh):
    placed = (
        P(None, None, ("surf", "recv"), "shot"),
        P(None, None, ("surf", "shot"), "recv"),
        P("shot"),
        P("recv"),
        P("shot"),
        P("recv"),
    )
    return jax.shard_map(
        lambda *args: predict(*args)[None],
        mesh=mesh,
        in_specs=placed,
        out_specs=P("surf", None, "shot", "recv"),
        check_vma=False,
    )
```
